32 devices in a mesh: resp: 2 (over y), item: 16 (over z, x, core).
Axes of the slice: x: 2, y: 2, z: 4, core: 2. Of those that a mesh axis runs over, the one named last changes fastest.
Arguments:
- coupling: bfloat16 [2, 4096, 2048], P('resp', 'item'), may hold values from -6 to 6
- noise: bfloat16 [2, 4096, 2048], P('resp', 'item'), may hold values from -6 to 6
- bias: float32 [16, 256], P('item', 'resp'), may hold values from -4 to 4
- responses: int32 [1024, 4096], P(None, 'item'), may hold values 0 or 1
- indices: int32 [512], replicated, may hold values from 0 to 1023
Outputs:
- new_coupling: bfloat16 [2, 4096, 2048], P('resp', 'item')
The draws below stay inside these ranges and needn't reach their ends.
All inputs are finite; a program needn't handle non-finite values. No bound on the sum of `responses` on one device may be relied on, other than what follows from the above.
Results may differ from the reference program's by a relative error of at most 0.0035.
Values may be sent and summed in bfloat16 or wider, within the bound.
No kernel may reach another device: no remote copies, remote signals or barrier semaphores. Data moves between devices by JAX's collectives and lax.ppermute only.
A program may use at most 64 MiB of HBM per device.

```python
import math
import jax
import jax.numpy as jnp
from jax import lax

ITEM_DEV = 256
BATCH = 512
ITEMS = 4096
SUB = 128
POOL = 1024
N_RESP = 2
N_ITEM = 16


def touch_ends(entries, own_key, smallest, top_value):
    longest = entries.shape.index(max(entries.shape))
    spots = []
    for shift in (0, 1):
        where = [jax.random.randint(jax.random.fold_in(own_key, axis), (), 0, length) for axis, length in enumerate(entries.shape)]
        where[longest] = (where[longest] + shift) % entries.shape[longest]
        spots.append(tuple(where))
    return entries.at[spots[0]].set(smallest).at[spots[1]].set(top_value)


def raised(result, rng, source, target, shards_of, factor):
    owner, partner = [(jnp.arange(result.shape[dim]) // (result.shape[dim] // shards_of)).reshape([-1 if axis == dim else 1 for axis in range(result.ndim)]) for dim in (source, target)]
    chosen = jax.random.permutation(rng, shards_of)[partner]
    strong = (owner == chosen) | (owner == (partner + shards_of // 2) % shards_of)
    return jnp.where(strong, factor * result, result)


def levels(rng, shape, shards, low, largest):
    gain = 1.0
    for dim, blocks in shards:
        heights = jax.random.uniform(jax.random.fold_in(jax.random.fold_in(rng, 6), dim), (blocks,), jnp.float32, low / len(shards), largest / len(shards))
        gain = gain * jnp.repeat(jnp.exp(heights), shape[dim] // blocks).reshape((-1,) + (1,) * (len(shape) - 1 - dim))
    return gain


def gaussian(rng, dims, scale, reach, shards=(), held_as=jnp.bfloat16):
    array = jax.random.normal(rng, dims, jnp.float32) * scale
    if len(shards) > 0:
        array = levels(rng, dims, shards, -0.22, 0.18) * array
    return jnp.clip(array, min=-reach, max=reach).astype(held_as)


def heavy_noise(stream_key, dims, scale, limit, pieces, heavy, kind=jnp.bfloat16):
    drawn = scale * jax.random.normal(stream_key, dims, jnp.float32)
    if pieces:
        drawn = drawn * levels(stream_key, dims, pieces, -0.22, 0.18)
    return jnp.clip(raised(drawn, jax.random.fold_in(stream_key, 3), *heavy), -limit, limit).astype(kind)


def setup_inputs(seed: int = 0) -> dict:
    keys = jax.random.split(jax.random.key(seed), 6)
    coupling = heavy_noise(keys[0], (N_RESP, ITEMS, N_ITEM * SUB), 1.0, 6.0, ((0, 2), (1, 16)), (1, 2, 16, 2.0))
    noise = gaussian(keys[1], (N_RESP, ITEMS, N_ITEM * SUB), 1.0, 6.0, ((0, 2), (1, 16)))
    bias = gaussian(keys[2], (N_ITEM, ITEM_DEV), 0.8, 4.0, ((0, 16), (1, 2)), jnp.float32)
    responses = touch_ends((jax.random.randint(keys[3], (POOL, ITEMS), 0, 2) < 1).astype(jnp.int32), jax.random.fold_in(keys[3], 1), 0, 1)
    indices = touch_ends(jax.random.randint(keys[4], (BATCH,), 0, POOL), jax.random.fold_in(keys[4], 1), 0, POOL - 1).astype(jnp.int32)
    return dict(coupling=coupling, noise=noise, bias=bias, responses=responses, indices=indices)


DRIFT = 0.01
DATA_RATIO = 900.0
NOISE_SCALE = math.sqrt(0.02)

def reference(coupling, noise, bias, responses, indices):
    sub_len = ITEM_DEV // N_RESP
    width = N_ITEM * sub_len
    inv_root = 1.0 / math.sqrt(ITEMS)
    chosen = responses[indices]
    spin_vals = (2 * chosen - 1).astype(jnp.bfloat16)
    answers = chosen.astype(jnp.float32)
    bias_flat = bias.reshape(ITEMS)
    position = jnp.arange(width, dtype=jnp.int32)
    resp_ids = jnp.arange(N_RESP, dtype=jnp.int32)
    item_rows = jnp.arange(ITEMS, dtype=jnp.int32)

    def columns_of(resp_idx):
        return position // sub_len * ITEM_DEV + resp_idx * sub_len + position % sub_len

    def residual_block(args):
        couple, resp_idx = args
        cols = columns_of(resp_idx)
        raw = jnp.dot(spin_vals, couple, preferred_element_type=jnp.float32)
        self_weight = couple[cols, position].astype(jnp.float32)
        own_spin = spin_vals[:, cols].astype(jnp.float32)
        fields = (raw - own_spin * self_weight[None, :]) * inv_root + bias_flat[cols][None, :]
        return (answers[:, cols] - jax.nn.sigmoid(fields)).astype(jnp.bfloat16)
    blocks = lax.map(residual_block, (coupling, resp_ids))
    residual = blocks.reshape(N_RESP, BATCH, N_ITEM, sub_len).transpose(1, 2, 0, 3).reshape(BATCH, ITEMS)

    def update_block(args):
        couple, noise_block, resp_idx = args
        cols = columns_of(resp_idx)
        first = jnp.dot(spin_vals.T, residual[:, cols], preferred_element_type=jnp.float32)
        second = jnp.dot(residual.T, spin_vals[:, cols], preferred_element_type=jnp.float32)
        gradient = jnp.where(item_rows[:, None] == cols[None, :], jnp.float32(0.0), first + second) * inv_root
        current = couple.astype(jnp.float32)
        updated = current + DRIFT * (DATA_RATIO * gradient - current) + NOISE_SCALE * noise_block.astype(jnp.float32)
        return updated.astype(jnp.bfloat16)
    return lax.map(update_block, (coupling, noise, resp_ids))
```

```python
import functools
import math

import jax
import jax.numpy as jnp
from jax import lax
from jax.experimental import pallas as pl
from jax.experimental.pallas import tpu as pltpu
from jax.sharding import PartitionSpec as P

DRIFT = 0.01
DATA_RATIO = 900.0
NOISE_SCALE = math.sqrt(0.02)
NT = (((1,), (1,)), ((), ()))
TN = (((0,), (0,)), ((), ()))


def spins_kernel(index_ref, responses_ref, spins_ref):
    pool = responses_ref.shape[0]
    batch = index_ref.shape[1]
    row_ids = lax.broadcasted_iota(jnp.int32, (pool, batch), 0)
    picks = jnp.where(row_ids == index_ref[...], 1.0, 0.0).astype(jnp.bfloat16)
    pool_spins = (2 * responses_ref[...] - 1).astype(jnp.float32).astype(jnp.bfloat16)
    spins_ref[...] = lax.dot_general(
        pool_spins, picks, TN, preferred_element_type=jnp.float32
    ).astype(jnp.bfloat16)


def gather_spins(responses, indices):
    return pl.pallas_call(
        spins_kernel,
        out_shape=jax.ShapeDtypeStruct((responses.shape[1], indices.shape[0]), jnp.bfloat16),
        name="gather_spins",
    )(indices[None], responses)


def update_kernel(
    inv_root, place_ref, spin_ref, res_ref, all_res_ref, all_spin_ref, couple_ref, noise_ref, out_ref
):
    grad = lax.dot_general(
        spin_ref[...], all_res_ref[...], NT, preferred_element_type=jnp.float32
    ) + lax.dot_general(res_ref[...], all_spin_ref[...], NT, preferred_element_type=jnp.float32)
    rows, cols = grad.shape
    row_ids = lax.broadcasted_iota(jnp.int32, (rows, cols), 0)
    col_ids = lax.broadcasted_iota(jnp.int32, (rows, cols), 1) + pl.program_id(0) * cols
    own_start, sub_len, first_col = place_ref[0], place_ref[1], place_ref[2]
    on_diag = (
        (col_ids - first_col == row_ids - own_start)
        & (row_ids >= own_start)
        & (row_ids < own_start + sub_len)
    )
    grad = jnp.where(on_diag, 0.0, grad) * inv_root
    current = couple_ref[...].astype(jnp.float32)
    out_ref[...] = (
        current
        + DRIFT * (DATA_RATIO * grad - current)
        + NOISE_SCALE * noise_ref[...].astype(jnp.float32)
    ).astype(jnp.bfloat16)


def update(place, spins, res, all_res, all_spin, couple, noise, inv_root):
    rows, width = couple.shape
    batch = spins.shape[1]
    block = min(512, width)
    fixed = lambda shape: pl.BlockSpec(shape, lambda j: (0, 0))
    return pl.pallas_call(
        functools.partial(update_kernel, inv_root),
        grid=(width // block,),
        in_specs=[
            pl.BlockSpec(memory_space=pltpu.SMEM),
            fixed((rows, batch)),
            fixed((rows, batch)),
            pl.BlockSpec((block, batch), lambda j: (j, 0)),
            pl.BlockSpec((block, batch), lambda j: (j, 0)),
            pl.BlockSpec((rows, block), lambda j: (0, j)),
            pl.BlockSpec((rows, block), lambda j: (0, j)),
        ],
        out_specs=pl.BlockSpec((rows, block), lambda j: (0, j)),
        out_shape=jax.ShapeDtypeStruct((rows, width), jnp.bfloat16),
        name="update",
    )(place, spins, res, all_res, all_spin, couple, noise)


def shards(coupling, noise, bias, responses, indices):
    couple = coupling[0]
    item_dev = couple.shape[0]
    batch = indices.shape[0]
    n_resp = lax.axis_size("resp")
    n_item = lax.axis_size("item")
    sub_len = item_dev // n_resp
    n_far = n_item // 4
    inv_root = 1.0 / math.sqrt(item_dev * n_item)
    resp_idx = lax.axis_index("resp")
    item_idx = lax.axis_index("item")
    far_idx, near_idx, core_idx = item_idx // 4, item_idx // 2 % 2, item_idx % 2
    own_start = resp_idx * sub_len
    swap_core = [(i, i ^ 1) for i in range(n_item)]
    swap_near = [(i, i ^ 2) for i in range(n_item)]

    def half(blocks, axis, index):
        return lax.dynamic_index_in_dim(blocks, index, axis, keepdims=False)

    by_core = couple.reshape(item_dev, 2 * n_far, 2, sub_len)
    kept = half(by_core, 2, core_idx).reshape(item_dev, -1)
    given = half(by_core, 2, 1 - core_idx).reshape(item_dev, -1)
    got = lax.ppermute(given, "item", swap_core)

    spins = gather_spins(responses, indices)
    peer_spins = lax.ppermute(spins, "item", swap_core)
    own_spins = lax.dynamic_slice_in_dim(spins, own_start, sub_len, 0)
    all_spins = lax.all_gather(own_spins, "item", axis=0, tiled=True)

    partial = lax.dot_general(
        kept, spins, TN, preferred_element_type=jnp.float32
    ) + lax.dot_general(got, peer_spins, TN, preferred_element_type=jnp.float32)

    by_near = partial.reshape(n_far, 2, sub_len, batch)
    sent = half(by_near, 1, 1 - near_idx).astype(jnp.bfloat16)
    held = half(by_near, 1, near_idx) + lax.ppermute(sent, "item", swap_near).astype(jnp.float32)
    total = half(held, 0, far_idx)
    for step in range(1, n_far):
        ring = [(i, (i + 4 * step) % n_item) for i in range(n_item)]
        piece = half(held, 0, (far_idx + step) % n_far).astype(jnp.bfloat16)
        total = total + lax.ppermute(piece, "item", ring).astype(jnp.float32)

    diag_block = lax.dynamic_slice(couple, (own_start, item_idx * sub_len), (sub_len, sub_len))
    row_ids = lax.broadcasted_iota(jnp.int32, (sub_len, sub_len), 0)
    col_ids = lax.broadcasted_iota(jnp.int32, (sub_len, sub_len), 1)
    self_weight = jnp.sum(
        jnp.where(row_ids == col_ids, diag_block.astype(jnp.float32), 0.0), axis=1, keepdims=True
    )
    own_spin = own_spins.astype(jnp.float32)
    fields = (total - self_weight * own_spin) * inv_root + bias[0][:, None]
    residual = (0.5 * (own_spin + 1.0) - jax.nn.sigmoid(fields)).astype(jnp.bfloat16)

    all_res = lax.all_gather(residual, "item", axis=0, tiled=True)
    row_res = lax.dynamic_update_slice_in_dim(
        jnp.zeros((item_dev, batch), jnp.bfloat16), residual, own_start, 0
    )
    for step in range(1, n_resp):
        ring = [(i, (i + step) % n_resp) for i in range(n_resp)]
        came = lax.ppermute(residual, "resp", ring)
        source = (resp_idx - step) % n_resp
        row_res = lax.dynamic_update_slice_in_dim(row_res, came, source * sub_len, 0)

    place = jnp.stack([own_start, jnp.int32(sub_len), item_idx * sub_len]).astype(jnp.int32)
    return update(place, spins, row_res, all_res, all_spins, couple, noise[0], inv_root)[None]


def solution(mesh):
    return jax.shard_map(
        shards,
        mesh=mesh,
        in_specs=(
            P("resp", "item", None),
            P("resp", "item", None),
            P("item", "resp"),
            P(None, "item"),
            P(),
        ),
        out_specs=P("resp", "item", None),
        check_vma=False,
    )
```

```python
import functools
import math

import jax
import jax.numpy as jnp
from jax import lax
from jax.experimental import pallas as pl
from jax.experimental.pallas import tpu as pltpu
from jax.sharding import PartitionSpec as P

DRIFT = 0.01
DATA_RATIO = 900.0
NOISE_SCALE = math.sqrt(0.02)
NT = (((1,), (1,)), ((), ()))
TN = (((0,), (0,)), ((), ()))


def spins_kernel(index_ref, responses_ref, spins_ref):
    pool = responses_ref.shape[0]
    batch = index_ref.shape[1]
    row_ids = lax.broadcasted_iota(jnp.int32, (pool, batch), 0)
    picks = jnp.where(row_ids == index_ref[...], 1.0, 0.0).astype(jnp.bfloat16)
    pool_spins = (2 * responses_ref[...] - 1).astype(jnp.float32).astype(jnp.bfloat16)
    spins_ref[...] = lax.dot_general(
        pool_spins, picks, TN, preferred_element_type=jnp.float32
    ).astype(jnp.bfloat16)


def gather_spins(responses, indices):
    return pl.pallas_call(
        spins_kernel,
        out_shape=jax.ShapeDtypeStruct((responses.shape[1], indices.shape[0]), jnp.bfloat16),
        name="gather_spins",
    )(indices[None], responses)


def block_rows(block, sub_len):
    return pl.ds(pl.multiple_of(block * sub_len, sub_len), sub_len)


def off_diag(grad, place_ref, sub_len):
    row_ids = lax.broadcasted_iota(jnp.int32, grad.shape, 0) - place_ref[0]
    col_ids = lax.broadcasted_iota(jnp.int32, grad.shape, 1) - place_ref[1] * sub_len
    on_diag = (col_ids == row_ids) & (row_ids >= 0) & (row_ids < sub_len)
    return jnp.where(on_diag, 0.0, grad)


def base_kernel(inv_root, place_ref, res_ref, *refs):
    *spin_refs, couple_ref, noise_ref, base_ref, spin_scr = refs
    sub_len = spin_refs[0].shape[1]
    step = pl.program_id(0)
    for low in range(8):
        block = spin_refs[low % 4][2 * step + low // 4]
        spin_scr[block_rows(place_ref[1] ^ low, sub_len), :] = block
    grad = lax.dot_general(res_ref[...], spin_scr[...], NT, preferred_element_type=jnp.float32)
    grad = jnp.where(step == 0, off_diag(grad, place_ref, sub_len), grad) * inv_root
    current = couple_ref[...].astype(jnp.float32)
    base_ref[...] = (
        current
        + DRIFT * (DATA_RATIO * grad - current)
        + NOISE_SCALE * noise_ref[...].astype(jnp.float32)
    )


def base_update(place, res, spin_blocks, couple, noise, inv_root):
    rows, width = couple.shape
    batch = res.shape[1]
    n_far, sub_len = spin_blocks[0].shape[0] // 2, spin_blocks[0].shape[1]
    columns = pl.BlockSpec((rows, 8 * sub_len), lambda j, place: (0, place[2] ^ j))
    whole = lambda array: pl.BlockSpec(array.shape, lambda j, place: (0,) * array.ndim)
    return pl.pallas_call(
        functools.partial(base_kernel, inv_root),
        grid_spec=pltpu.PrefetchScalarGridSpec(
            num_scalar_prefetch=1,
            grid=(n_far,),
            in_specs=[whole(res)] + [whole(x) for x in spin_blocks] + [columns, columns],
            out_specs=columns,
            scratch_shapes=[pltpu.VMEM((8 * sub_len, batch), jnp.bfloat16)],
        ),
        out_shape=jax.ShapeDtypeStruct((rows, width), jnp.float32),
        name="base_update",
    )(place, res, *spin_blocks, couple, noise)


def add_kernel(inv_root, step, place_ref, spin_ref, *refs):
    res_refs, peer_ref, base_ref, out_ref, res_scr = refs[:4], refs[4], refs[5], refs[-2], refs[-1]
    sub_len = res_refs[0].shape[0]
    for pair in range(4):
        low = 2 * pair
        res_scr[block_rows(place_ref[1] ^ low, sub_len), :] = res_refs[pair][...]
        res_scr[block_rows(place_ref[1] ^ (low + 1), sub_len), :] = peer_ref[pair]
    grad = lax.dot_general(spin_ref[...], res_scr[...], NT, preferred_element_type=jnp.float32)
    if step == 0:
        grad = off_diag(grad, place_ref, sub_len)
    out_ref[...] = (base_ref[...] + (DRIFT * DATA_RATIO * inv_root) * grad).astype(jnp.bfloat16)


def add_update(place, spins, blocks, peers, base, out, step, inv_root):
    rows, width = base.shape
    sub_len, batch = blocks[0].shape
    columns = pl.BlockSpec((rows, 8 * sub_len), lambda j, place: (0, place[2] ^ step))
    whole = lambda array: pl.BlockSpec(array.shape, lambda j, place: (0,) * array.ndim)
    operands = [spins, *blocks, peers]
    specs = [whole(x) for x in operands] + [columns]
    operands.append(base)
    aliases = {}
    if out is not None:
        aliases = {1 + len(operands): 0}
        operands.append(out)
        specs.append(pl.BlockSpec(memory_space=pl.ANY))
    return pl.pallas_call(
        functools.partial(add_kernel, inv_root, step),
        grid_spec=pltpu.PrefetchScalarGridSpec(
            num_scalar_prefetch=1,
            grid=(1,),
            in_specs=specs,
            out_specs=columns,
            scratch_shapes=[pltpu.VMEM((8 * sub_len, batch), jnp.bfloat16)],
        ),
        out_shape=jax.ShapeDtypeStruct((rows, width), jnp.bfloat16),
        input_output_aliases=aliases,
        name="add_update",
    )(place, *operands)


def shards(coupling, noise, bias, responses, indices):
    couple = coupling[0]
    item_dev = couple.shape[0]
    batch = indices.shape[0]
    n_resp = lax.axis_size("resp")
    n_item = lax.axis_size("item")
    sub_len = item_dev // n_resp
    n_far = n_item // 4
    inv_root = 1.0 / math.sqrt(item_dev * n_item)
    resp_idx = lax.axis_index("resp")
    item_idx = lax.axis_index("item")
    far_idx, near_idx, core_idx = item_idx // 4, item_idx // 2 % 2, item_idx % 2
    own_start = resp_idx * sub_len

    def swap(array, bits):
        return lax.ppermute(array, "item", [(i, i ^ bits) for i in range(n_item)])

    def half(blocks, axis, index):
        return lax.dynamic_index_in_dim(blocks, index, axis, keepdims=False)

    by_core = couple.reshape(item_dev, 2 * n_far, 2, sub_len)
    kept = half(by_core, 2, core_idx).reshape(item_dev, -1)
    given = half(by_core, 2, 1 - core_idx).reshape(item_dev, -1)
    got = swap(given, 1)

    spins = gather_spins(responses, indices)
    peer_spins = swap(spins, 1)
    own_spins = lax.dynamic_slice_in_dim(spins, own_start, sub_len, 0)

    partial = lax.dot_general(
        kept, spins, TN, preferred_element_type=jnp.float32
    ) + lax.dot_general(got, peer_spins, TN, preferred_element_type=jnp.float32)

    by_near = partial.reshape(n_far, 2, sub_len, batch)
    sent = half(by_near, 1, 1 - near_idx).astype(jnp.bfloat16)
    held = half(by_near, 1, near_idx) + swap(sent, 2).astype(jnp.float32)
    total = half(held, 0, far_idx)
    for step in range(1, n_far):
        piece = half(held, 0, far_idx ^ step).astype(jnp.bfloat16)
        total = total + swap(piece, 4 * step).astype(jnp.float32)

    line_spins = jnp.stack([own_spins] + [swap(own_spins, 4 * step) for step in range(1, n_far)])
    near_spins = swap(line_spins, 2)
    spin_blocks = [line_spins, swap(line_spins, 1), near_spins, swap(near_spins, 1)]

    diag_block = lax.dynamic_slice(couple, (own_start, item_idx * sub_len), (sub_len, sub_len))
    row_ids = lax.broadcasted_iota(jnp.int32, (sub_len, sub_len), 0)
    col_ids = lax.broadcasted_iota(jnp.int32, (sub_len, sub_len), 1)
    self_weight = jnp.sum(
        jnp.where(row_ids == col_ids, diag_block.astype(jnp.float32), 0.0), axis=1, keepdims=True
    )
    own_spin = own_spins.astype(jnp.float32)
    fields = (total - self_weight * own_spin) * inv_root + bias[0][:, None]
    residual = (0.5 * (own_spin + 1.0) - jax.nn.sigmoid(fields)).astype(jnp.bfloat16)

    row_res = lax.dynamic_update_slice_in_dim(
        jnp.zeros((item_dev, batch), jnp.bfloat16), residual, own_start, 0
    )
    for step in range(1, n_resp):
        ring = [(i, (i + step) % n_resp) for i in range(n_resp)]
        came = lax.ppermute(residual, "resp", ring)
        source = (resp_idx - step) % n_resp
        row_res = lax.dynamic_update_slice_in_dim(row_res, came, source * sub_len, 0)

    place = jnp.stack([own_start, item_idx % 8, item_idx // 8]).astype(jnp.int32)
    base = base_update(place, row_res, spin_blocks, couple, noise[0], inv_root)
    out = None
    for step in range(n_item // 8):
        start = swap(residual, 8 * step) if step else residual
        blocks = [start] + [swap(start, bits) for bits in (2, 4, 6)]
        out = add_update(place, spins, blocks, swap(jnp.stack(blocks), 1), base, out, step, inv_root)
    return out[None]


def solution(mesh):
    return jax.shard_map(
        shards,
        mesh=mesh,
        in_specs=(
            P("resp", "item", None),
            P("resp", "item", None),
            P("item", "resp"),
            P(None, "item"),
            P(),
        ),
        out_specs=P("resp", "item", None),
        check_vma=False,
    )
```

```python
import math

import jax
import jax.numpy as jnp
from jax import lax
from jax.sharding import PartitionSpec as P

DRIFT = 0.01
DATA_RATIO = 900.0
NOISE_SCALE = math.sqrt(0.02)
NT = (((1,), (1,)), ((), ()))
TN = (((0,), (0,)), ((), ()))


def shards(coupling, noise, bias, responses, indices):
    couple = coupling[0]
    item_dev = couple.shape[0]
    pool, batch = responses.shape[0], indices.shape[0]
    n_resp = lax.axis_size("resp")
    n_item = lax.axis_size("item")
    sub_len = item_dev // n_resp
    n_line = n_item // 4
    width = 8 * sub_len
    inv_root = 1.0 / math.sqrt(item_dev * n_item)
    resp_idx = lax.axis_index("resp")
    item_idx = lax.axis_index("item")
    line_idx, near_idx, core_idx = item_idx // 4, item_idx // 2 % 2, item_idx % 2
    low_idx, high_idx = item_idx % 8, item_idx // 8
    own_start = resp_idx * sub_len

    def swap(array, bits):
        return lax.ppermute(array, "item", [(i, i ^ bits) for i in range(n_item)])

    def take_rows(array, index, blocks, length):
        parts = array.reshape(-1, blocks, length, array.shape[1])
        part = lax.dynamic_index_in_dim(parts, index, 1, keepdims=False)
        return part.reshape(-1, array.shape[1])

    def in_order(blocks):
        joined = jnp.zeros((8, sub_len, batch), jnp.bfloat16)
        for low, block in enumerate(blocks):
            joined = lax.dynamic_update_index_in_dim(joined, block, low_idx ^ low, 0)
        return joined.reshape(width, batch)

    by_core = couple.reshape(item_dev, -1, 2, sub_len)
    kept = lax.dynamic_index_in_dim(by_core, core_idx, 2, keepdims=False)
    given = lax.dynamic_index_in_dim(by_core, 1 - core_idx, 2, keepdims=False)
    got = swap(given.reshape(item_dev, -1), 1)
    kept = kept.reshape(item_dev, -1)

    pool_ids = lax.broadcasted_iota(jnp.int32, (pool, batch), 0)
    picks = (pool_ids == indices[None]).astype(jnp.bfloat16)
    pool_spins = (2 * responses - 1).astype(jnp.bfloat16)
    spins = lax.dot_general(pool_spins, picks, TN, preferred_element_type=jnp.float32)
    spins = spins.astype(jnp.bfloat16)
    peer_spins = swap(spins, 1)
    own_spins = lax.dynamic_slice_in_dim(spins, own_start, sub_len, 0)

    partial = lax.dot_general(
        kept, spins, TN, preferred_element_type=jnp.float32
    ) + lax.dot_general(got, peer_spins, TN, preferred_element_type=jnp.float32)

    came = swap(take_rows(partial, 1 - near_idx, 2, sub_len).astype(jnp.bfloat16), 2)
    line = [own_spins] + [swap(own_spins, 4 * step) for step in range(1, n_line)]
    came, line = lax.optimization_barrier((came, line))
    held = take_rows(partial, near_idx, 2, sub_len) + came.astype(jnp.float32)
    pieces = [
        swap(take_rows(held, line_idx ^ step, n_line, sub_len).astype(jnp.bfloat16), 4 * step)
        for step in range(1, n_line)
    ]
    line_spins = jnp.concatenate(line)
    near_spins, peer_line = swap(line_spins, 2), swap(line_spins, 1)
    pieces, near_spins, peer_line = lax.optimization_barrier((pieces, near_spins, peer_line))
    spin_groups = [line_spins, peer_line, near_spins, swap(near_spins, 1)]
    total = take_rows(held, line_idx, n_line, sub_len)
    for piece in pieces:
        total = total + piece.astype(jnp.float32)

    diag_block = lax.dynamic_slice(couple, (own_start, item_idx * sub_len), (sub_len, sub_len))
    row_ids = lax.broadcasted_iota(jnp.int32, (sub_len, sub_len), 0)
    col_ids = lax.broadcasted_iota(jnp.int32, (sub_len, sub_len), 1)
    self_weight = jnp.sum(
        jnp.where(row_ids == col_ids, diag_block.astype(jnp.float32), 0.0), axis=1, keepdims=True
    )
    own_spin = own_spins.astype(jnp.float32)
    fields = (total - self_weight * own_spin) * inv_root + bias[0][:, None]
    residual = (0.5 * (own_spin + 1.0) - jax.nn.sigmoid(fields)).astype(jnp.bfloat16)

    row_res = lax.dynamic_update_slice_in_dim(
        jnp.zeros((item_dev, batch), jnp.bfloat16), residual, own_start, 0
    )
    for step in range(1, n_resp):
        ring = [(i, (i + step) % n_resp) for i in range(n_resp)]
        other = lax.ppermute(residual, "resp", ring)
        source = (resp_idx - step) % n_resp
        row_res = lax.dynamic_update_slice_in_dim(row_res, other, source * sub_len, 0)

    row_ids = lax.broadcasted_iota(jnp.int32, (item_dev, width), 0) - own_start
    col_ids = lax.broadcasted_iota(jnp.int32, (item_dev, width), 1) - low_idx * sub_len
    on_diag = (row_ids == col_ids) & (row_ids >= 0) & (row_ids < sub_len)

    def product(left, right, step):
        grad = lax.dot_general(left, right, NT, preferred_element_type=jnp.float32)
        return jnp.where(on_diag, 0.0, grad) if step == 0 else grad

    out = jnp.zeros(couple.shape, jnp.bfloat16)
    for step in range(n_item // 8):
        start = swap(residual, 8 * step) if step else residual
        blocks = [start] + [swap(start, bits) for bits in (2, 4, 6)]
        peers = swap(jnp.stack(blocks), 1)
        all_res = in_order([x for pair in zip(blocks, peers) for x in pair])
        all_spins = in_order(
            [
                lax.slice_in_dim(group, k * sub_len, (k + 1) * sub_len, axis=0)
                for k in (2 * step, 2 * step + 1)
                for group in spin_groups
            ]
        )
        first_col = (high_idx ^ step) * width
        current = lax.dynamic_slice_in_dim(couple, first_col, width, 1).astype(jnp.float32)
        shake = lax.dynamic_slice_in_dim(noise[0], first_col, width, 1).astype(jnp.float32)
        mirror = product(row_res, all_spins, step) * inv_root
        base = current + DRIFT * (DATA_RATIO * mirror - current) + NOISE_SCALE * shake
        base = lax.optimization_barrier(base)
        part = base + (DRIFT * DATA_RATIO * inv_root) * product(spins, all_res, step)
        out = lax.dynamic_update_slice_in_dim(out, part.astype(jnp.bfloat16), first_col, 1)
    return out[None]


def solution(mesh):
    return jax.shard_map(
        shards,
        mesh=mesh,
        in_specs=(
            P("resp", "item", None),
            P("resp", "item", None),
            P("item", "resp"),
            P(None, "item"),
            P(),
        ),
        out_specs=P("resp", "item", None),
        check_vma=False,
    )
```

```python
import math

import jax
import jax.numpy as jnp
from jax import lax
from jax.sharding import PartitionSpec as P

DRIFT = 0.01
DATA_RATIO = 900.0
NOISE_SCALE = math.sqrt(0.02)
NT = (((1,), (1,)), ((), ()))
TN = (((0,), (0,)), ((), ()))


def shards(coupling, noise, bias, responses, indices):
    couple = coupling[0]
    item_dev = couple.shape[0]
    pool, batch = responses.shape[0], indices.shape[0]
    n_resp = lax.axis_size("resp")
    n_item = lax.axis_size("item")
    sub_len = item_dev // n_resp
    n_line = n_item // 4
    width = 8 * sub_len
    n_high = n_item // 8
    inv_root = 1.0 / math.sqrt(item_dev * n_item)
    resp_idx = lax.axis_index("resp")
    item_idx = lax.axis_index("item")

    core_idx, near_idx, line_idx, high_idx = item_idx % 2, item_idx // 2 % 2, item_idx // 4, item_idx // 8
    where = dict(
        core=core_idx,
        other_core=1 - core_idx,
        near=near_idx,
        other_near=1 - near_idx,
        line=[line_idx ^ step for step in range(n_line)],
        quad=[item_idx // 2 % 4 ^ step for step in range(4)],
        high=[high_idx ^ step for step in range(n_high)],
        is_high=[[high_idx ^ step == block for block in range(n_high)] for step in range(n_high)],
        source=[(resp_idx - step) % n_resp for step in range(n_resp)],
        own_start=resp_idx * sub_len,
        item_col=item_idx * sub_len,
        low_col=item_idx % 8 * sub_len,
    )
    indices, where = lax.optimization_barrier((indices, where))
    own_start = where["own_start"]

    def swap(array, bits):
        return lax.ppermute(array, "item", [(i, i ^ bits) for i in range(n_item)])

    def take(array, index, axis):
        return lax.dynamic_index_in_dim(array, index, axis, False, allow_negative_indices=False)

    def put_at(array, part, *starts):
        starts = starts + (0,) * (array.ndim - len(starts))
        return lax.dynamic_update_slice(array, part, starts, allow_negative_indices=False)

    by_core = couple.reshape(item_dev, -1, 2, sub_len)
    kept = take(by_core, where["core"], 2).reshape(item_dev, -1)
    given = take(by_core, where["other_core"], 2).reshape(item_dev, -1)
    got = swap(given, 1)

    pool_ids = lax.broadcasted_iota(jnp.int32, (pool, batch), 0)
    picks = (pool_ids == indices[None]).astype(jnp.bfloat16)
    pool_spins = (2 * responses - 1).astype(jnp.bfloat16)
    spins = lax.dot_general(pool_spins, picks, TN, preferred_element_type=jnp.float32)
    spins = spins.astype(jnp.bfloat16)
    peer_spins = swap(spins, 1)
    own_spins = take(spins.reshape(n_resp, sub_len, batch), where["source"][0], 0)

    partial = lax.dot_general(
        kept, spins, TN, preferred_element_type=jnp.float32
    ) + lax.dot_general(got, peer_spins, TN, preferred_element_type=jnp.float32)

    by_near = partial.reshape(n_line, 2, sub_len, batch)
    sent = take(by_near, where["other_near"], 1).astype(jnp.bfloat16)
    sent, own_spins = lax.optimization_barrier((sent, own_spins))
    came = swap(sent, 2)
    line = [swap(own_spins, 4 * step) for step in range(1, n_line)]
    came, line = lax.optimization_barrier((came, line))
    held = take(by_near, where["near"], 1) + came.astype(jnp.float32)
    pieces = [take(held, index, 0).astype(jnp.bfloat16) for index in where["line"][1:]]
    line_spins = jnp.zeros((n_line, sub_len, batch), jnp.bfloat16)
    for index, block in zip(where["line"], [own_spins] + line):
        line_spins = put_at(line_spins, block[None], index)
    pieces, line_spins = lax.optimization_barrier((pieces, line_spins))
    pieces = [swap(piece, 4 * step) for step, piece in enumerate(pieces, 1)]
    near_spins, peer_line = swap(line_spins, 2), swap(line_spins, 1)
    pieces, near_spins, peer_line = lax.optimization_barrier((pieces, near_spins, peer_line))
    all_spins = jnp.zeros((n_line, 2, 2, sub_len, batch), jnp.bfloat16)
    for near, core, group in (
        ("near", "core", line_spins),
        ("near", "other_core", peer_line),
        ("other_near", "core", near_spins),
        ("other_near", "other_core", swap(near_spins, 1)),
    ):
        all_spins = put_at(all_spins, group[:, None, None], 0, where[near], where[core])
    all_spins = all_spins.reshape(n_high, width, batch)
    total = take(held, where["line"][0], 0)
    for piece in pieces:
        total = total + piece.astype(jnp.float32)

    row_ids = lax.broadcasted_iota(jnp.int32, couple.shape, 0) - own_start
    col_ids = lax.broadcasted_iota(jnp.int32, couple.shape, 1) - where["item_col"]
    self_weight = jnp.sum(
        jnp.where(row_ids == col_ids, couple.astype(jnp.float32), 0.0), axis=1
    ).reshape(n_resp, sub_len, 1)
    self_weight = take(self_weight, where["source"][0], 0)
    own_spin = own_spins.astype(jnp.float32)
    fields = (total - self_weight * own_spin) * inv_root + bias[0][:, None]
    residual = (0.5 * (own_spin + 1.0) - jax.nn.sigmoid(fields)).astype(jnp.bfloat16)

    far = [swap(residual, 8 * step) for step in range(1, n_high)]
    others = []
    for step in range(1, n_resp):
        ring = [(i, (i + step) % n_resp) for i in range(n_resp)]
        others.append(lax.ppermute(residual, "resp", ring))
    near = [swap(residual, bits) for bits in (2, 4, 6)]
    far, others, near = lax.optimization_barrier((far, others, near))
    row_res = jnp.zeros((n_resp, sub_len, batch), jnp.bfloat16)
    for index, block in zip(where["source"], [residual] + others):
        row_res = put_at(row_res, block[None], index)
    row_res = row_res.reshape(item_dev, batch)

    row_ids = lax.broadcasted_iota(jnp.int32, (item_dev, width), 0) - own_start
    col_ids = lax.broadcasted_iota(jnp.int32, (item_dev, width), 1) - where["low_col"]
    on_diag = (row_ids == col_ids) & (row_ids >= 0) & (row_ids < sub_len)

    def product(left, right, step):
        grad = lax.dot_general(left, right, NT, preferred_element_type=jnp.float32)
        return jnp.where(on_diag, 0.0, grad) if step == 0 else grad

    def pick(blocks, step):
        picked = blocks[0]
        for index in range(1, n_high):
            picked = jnp.where(where["is_high"][step][index], blocks[index], picked)
        return picked

    def pick_part(parts, block):
        picked = parts[0]
        for step in range(1, n_high):
            picked = jnp.where(where["is_high"][step][block], parts[step], picked)
        return picked

    couple_blocks = jnp.split(couple, n_high, axis=1)
    noise_blocks = jnp.split(noise[0], n_high, axis=1)
    parts = []
    for step in range(n_high):
        current = pick(couple_blocks, step).astype(jnp.float32)
        shake = pick(noise_blocks, step).astype(jnp.float32)
        mirror = product(row_res, take(all_spins, where["high"][step], 0), step) * inv_root
        base = current + DRIFT * (DATA_RATIO * mirror - current) + NOISE_SCALE * shake

        if step:
            blocks = [far[step - 1]] + [swap(far[step - 1], bits) for bits in (2, 4, 6)]
        else:
            blocks = [residual] + near
        if step == n_high - 1:
            blocks, base, parts = lax.optimization_barrier((blocks, base, parts))
        quad = jnp.zeros((4, sub_len, batch), jnp.bfloat16)
        for index, block in zip(where["quad"], blocks):
            quad = put_at(quad, block[None], index)
        peers = swap(quad, 1)
        all_res = jnp.zeros((4, 2, sub_len, batch), jnp.bfloat16)
        all_res = put_at(all_res, quad[:, None], 0, where["core"])
        all_res = put_at(all_res, peers[:, None], 0, where["other_core"])
        part = product(spins, all_res.reshape(width, batch), step)
        part = base + (DRIFT * DATA_RATIO * inv_root) * part
        parts.append(part.astype(jnp.bfloat16))
    return jnp.concatenate([pick_part(parts, i) for i in range(n_high)], axis=1)[None]


def solution(mesh):
    return jax.shard_map(
        shards,
        mesh=mesh,
        in_specs=(
            P("resp", "item", None),
            P("resp", "item", None),
            P("item", "resp"),
            P(None, "item"),
            P(),
        ),
        out_specs=P("resp", "item", None),
        check_vma=False,
    )
```

```python
import math

import jax
import jax.numpy as jnp
from jax import lax
from jax.sharding import PartitionSpec as P

DRIFT = 0.01
DATA_RATIO = 900.0
NOISE_SCALE = math.sqrt(0.02)
NT = (((1,), (1,)), ((), ()))
TN = (((0,), (0,)), ((), ()))


def shards(coupling, noise, bias, responses, indices):
    couple = coupling[0]
    item_dev = couple.shape[0]
    pool, batch = responses.shape[0], indices.shape[0]
    n_resp = lax.axis_size("resp")
    n_item = lax.axis_size("item")
    sub_len = item_dev // n_resp
    n_line = n_item // 4
    width = 8 * sub_len
    n_high = n_item // 8
    inv_root = 1.0 / math.sqrt(item_dev * n_item)
    resp_idx = lax.axis_index("resp")
    item_idx = lax.axis_index("item")

    core_idx, near_idx, line_idx, high_idx = item_idx % 2, item_idx // 2 % 2, item_idx // 4, item_idx // 8
    where = dict(
        core=core_idx,
        other_core=1 - core_idx,
        near=near_idx,
        other_near=1 - near_idx,
        line=[line_idx ^ step for step in range(n_line)],
        quad=[item_idx // 2 % 4 ^ step for step in range(4)],
        high=[high_idx ^ step for step in range(n_high)],
        is_high=[[high_idx ^ step == block for block in range(n_high)] for step in range(n_high)],
        source=[(resp_idx - step) % n_resp for step in range(n_resp)],
        own_start=resp_idx * sub_len,
        item_col=item_idx * sub_len,
        low_col=item_idx % 8 * sub_len,
    )
    indices, where = lax.optimization_barrier((indices, where))
    own_start = where["own_start"]

    def swap(array, bits):
        return lax.ppermute(array, "item", [(i, i ^ bits) for i in range(n_item)])

    def take(array, index, axis):
        return lax.dynamic_index_in_dim(array, index, axis, False, allow_negative_indices=False)

    def put_at(array, part, *starts):
        starts = starts + (0,) * (array.ndim - len(starts))
        return lax.dynamic_update_slice(array, part, starts, allow_negative_indices=False)

    by_core = couple.reshape(item_dev, -1, 2, sub_len)
    kept = take(by_core, where["core"], 2).reshape(item_dev, -1)
    given = take(by_core, where["other_core"], 2).reshape(item_dev, -1)
    got = swap(given, 1)

    pool_ids = lax.broadcasted_iota(jnp.int32, (pool, batch), 0)
    picks = (pool_ids == indices[None]).astype(jnp.bfloat16)
    pool_spins = (2 * responses - 1).astype(jnp.bfloat16)
    spins = lax.dot_general(pool_spins, picks, TN, preferred_element_type=jnp.float32)
    spins = spins.astype(jnp.bfloat16)
    peer_spins = swap(spins, 1)
    own_spins = take(spins.reshape(n_resp, sub_len, batch), where["source"][0], 0)

    partial = lax.dot_general(
        kept, spins, TN, preferred_element_type=jnp.float32
    ) + lax.dot_general(got, peer_spins, TN, preferred_element_type=jnp.float32)

    by_near = partial.reshape(n_line, 2, sub_len, batch)
    sent = take(by_near, where["other_near"], 1).astype(jnp.bfloat16)
    mine = take(by_near, where["near"], 1)
    sent, mine, own_spins = lax.optimization_barrier((sent, mine, own_spins))
    distant, close = list(range(2, n_line)), [1, 0]

    def across(steps):
        return jnp.stack([take(sent, where["line"][step], 0) for step in steps])

    def added(steps, came):
        kept = jnp.stack([take(mine, where["line"][step], 0) for step in steps])
        return kept + came.astype(jnp.float32)

    groups = lax.optimization_barrier((across(distant), across(close)))
    came = [swap(group, 2) for group in groups]
    line = [swap(own_spins, 4 * step) for step in range(1, n_line)]
    distant_sums = added(distant, came[0]).astype(jnp.bfloat16)
    pieces = [swap(block, 4 * step) for step, block in zip(distant, distant_sums)]
    came_close, _ = lax.optimization_barrier((came[1], distant_sums))
    close_sums = added(close, came_close)
    close_piece = swap(close_sums[0].astype(jnp.bfloat16), 4)
    line, _ = lax.optimization_barrier((line, close_sums))
    line_spins = jnp.zeros((n_line, sub_len, batch), jnp.bfloat16)
    for index, block in zip(where["line"], [own_spins] + line):
        line_spins = put_at(line_spins, block[None], index)
    near_spins, peer_line = swap(line_spins, 2), swap(line_spins, 1)
    total = close_sums[1]
    for piece in pieces:
        total = total + piece.astype(jnp.float32)
    total, near_spins, peer_line = lax.optimization_barrier((total, near_spins, peer_line))
    total = total + close_piece.astype(jnp.float32)
    all_spins = jnp.zeros((n_line, 2, 2, sub_len, batch), jnp.bfloat16)
    for near, core, group in (
        ("near", "core", line_spins),
        ("near", "other_core", peer_line),
        ("other_near", "core", near_spins),
        ("other_near", "other_core", swap(near_spins, 1)),
    ):
        all_spins = put_at(all_spins, group[:, None, None], 0, where[near], where[core])
    all_spins = all_spins.reshape(n_high, width, batch)
    row_ids = lax.broadcasted_iota(jnp.int32, couple.shape, 0) - own_start
    col_ids = lax.broadcasted_iota(jnp.int32, couple.shape, 1) - where["item_col"]
    self_weight = jnp.sum(
        jnp.where(row_ids == col_ids, couple.astype(jnp.float32), 0.0), axis=1
    ).reshape(n_resp, sub_len, 1)
    self_weight = take(self_weight, where["source"][0], 0)
    own_spin = own_spins.astype(jnp.float32)
    fields = (total - self_weight * own_spin) * inv_root + bias[0][:, None]
    residual = (0.5 * (own_spin + 1.0) - jax.nn.sigmoid(fields)).astype(jnp.bfloat16)

    far = [swap(residual, 8 * step) for step in range(1, n_high)]
    others = []
    for step in range(1, n_resp):
        ring = [(i, (i + step) % n_resp) for i in range(n_resp)]
        others.append(lax.ppermute(residual, "resp", ring))
    near = [swap(residual, bits) for bits in (2, 4, 6)]
    far, near[:2] = lax.optimization_barrier((far, near[:2]))
    row_res = jnp.zeros((n_resp, sub_len, batch), jnp.bfloat16)
    for index, block in zip(where["source"], [residual] + others):
        row_res = put_at(row_res, block[None], index)
    row_res = row_res.reshape(item_dev, batch)

    row_ids = lax.broadcasted_iota(jnp.int32, (item_dev, width), 0) - own_start
    col_ids = lax.broadcasted_iota(jnp.int32, (item_dev, width), 1) - where["low_col"]
    on_diag = (row_ids == col_ids) & (row_ids >= 0) & (row_ids < sub_len)

    def product(left, right, step):
        grad = lax.dot_general(left, right, NT, preferred_element_type=jnp.float32)
        return jnp.where(on_diag, 0.0, grad) if step == 0 else grad

    def pick(blocks, step):
        picked = blocks[0]
        for index in range(1, n_high):
            picked = jnp.where(where["is_high"][step][index], blocks[index], picked)
        return picked

    def pick_part(parts, block):
        picked = parts[0]
        for step in range(1, n_high):
            picked = jnp.where(where["is_high"][step][block], parts[step], picked)
        return picked

    couple_blocks = jnp.split(couple, n_high, axis=1)
    noise_blocks = jnp.split(noise[0], n_high, axis=1)
    parts = []
    for step in range(n_high):
        current = pick(couple_blocks, step).astype(jnp.float32)
        shake = pick(noise_blocks, step).astype(jnp.float32)
        mirror = product(row_res, take(all_spins, where["high"][step], 0), step) * inv_root
        base = current + DRIFT * (DATA_RATIO * mirror - current) + NOISE_SCALE * shake

        if step:
            blocks = [far[step - 1]] + [swap(far[step - 1], bits) for bits in (2, 4, 6)]
        else:
            blocks = [residual] + near
        if step == n_high - 1:
            blocks, base, parts = lax.optimization_barrier((blocks, base, parts))
        quad = jnp.zeros((4, sub_len, batch), jnp.bfloat16)
        for index, block in zip(where["quad"], blocks):
            quad = put_at(quad, block[None], index)
        peers = swap(quad, 1)
        all_res = jnp.zeros((4, 2, sub_len, batch), jnp.bfloat16)
        all_res = put_at(all_res, quad[:, None], 0, where["core"])
        all_res = put_at(all_res, peers[:, None], 0, where["other_core"])
        part = product(spins, all_res.reshape(width, batch), step)
        part = base + (DRIFT * DATA_RATIO * inv_root) * part
        parts.append(part.astype(jnp.bfloat16))
    return jnp.concatenate([pick_part(parts, i) for i in range(n_high)], axis=1)[None]


def solution(mesh):
    return jax.shard_map(
        shards,
        mesh=mesh,
        in_specs=(
            P("resp", "item", None),
            P("resp", "item", None),
            P("item", "resp"),
            P(None, "item"),
            P(),
        ),
        out_specs=P("resp", "item", None),
        check_vma=False,
    )
```

```python
import math

import jax
import jax.numpy as jnp
from jax import lax
from jax.sharding import PartitionSpec as P

DRIFT = 0.01
DATA_RATIO = 900.0
NOISE_SCALE = math.sqrt(0.02)
NT = (((1,), (1,)), ((), ()))
TN = (((0,), (0,)), ((), ()))


def shards(coupling, noise, bias, responses, indices):
    couple = coupling[0]
    item_dev = couple.shape[0]
    pool, batch = responses.shape[0], indices.shape[0]
    n_resp = lax.axis_size("resp")
    n_item = lax.axis_size("item")
    sub_len = item_dev // n_resp
    n_line = n_item // 4
    width = 8 * sub_len
    n_high = n_item // 8
    inv_root = 1.0 / math.sqrt(item_dev * n_item)
    resp_idx = lax.axis_index("resp")
    item_idx = lax.axis_index("item")

    core_idx, near_idx, line_idx, high_idx = item_idx % 2, item_idx // 2 % 2, item_idx // 4, item_idx // 8
    where = dict(
        core=core_idx,
        other_core=1 - core_idx,
        near=near_idx,
        other_near=1 - near_idx,
        line=[line_idx ^ step for step in range(n_line)],
        quad=[item_idx // 2 % 4 ^ step for step in range(4)],
        high=[high_idx ^ step for step in range(n_high)],
        is_high=[[high_idx ^ step == block for block in range(n_high)] for step in range(n_high)],
        source=[(resp_idx - step) % n_resp for step in range(n_resp)],
        own_start=resp_idx * sub_len,
        item_col=item_idx * sub_len,
        low_col=item_idx % 8 * sub_len,
    )
    indices, where = lax.optimization_barrier((indices, where))
    own_start = where["own_start"]

    def swap(array, bits):
        return lax.ppermute(array, "item", [(i, i ^ bits) for i in range(n_item)])

    def take(array, index, axis):
        return lax.dynamic_index_in_dim(array, index, axis, False, allow_negative_indices=False)

    def put_at(array, part, *starts):
        starts = starts + (0,) * (array.ndim - len(starts))
        return lax.dynamic_update_slice(array, part, starts, allow_negative_indices=False)

    by_core = couple.reshape(item_dev, -1, 2, sub_len)
    kept = take(by_core, where["core"], 2).reshape(item_dev, -1)
    given = take(by_core, where["other_core"], 2).reshape(item_dev, -1)
    got = swap(given, 1)

    pool_ids = lax.broadcasted_iota(jnp.int32, (pool, batch), 0)
    picks = (pool_ids == indices[None]).astype(jnp.bfloat16)
    pool_spins = (2 * responses - 1).astype(jnp.bfloat16)
    spins = lax.dot_general(pool_spins, picks, TN, preferred_element_type=jnp.float32)
    spins = spins.astype(jnp.bfloat16)
    peer_spins = swap(spins, 1)
    own_spins = take(spins.reshape(n_resp, sub_len, batch), where["source"][0], 0)

    partial = lax.dot_general(
        kept, spins, TN, preferred_element_type=jnp.float32
    ) + lax.dot_general(got, peer_spins, TN, preferred_element_type=jnp.float32)

    by_near = partial.reshape(n_line, 2, sub_len, batch)
    sent = take(by_near, where["other_near"], 1).astype(jnp.bfloat16)
    mine = take(by_near, where["near"], 1)
    sent, mine, own_spins = lax.optimization_barrier((sent, mine, own_spins))
    given_steps, kept_steps = list(range(1, n_line, 2)), list(range(0, n_line, 2))

    def across(steps):
        return jnp.stack([take(sent, where["line"][step], 0) for step in steps])

    def added(steps, came):
        kept = jnp.stack([take(mine, where["line"][step], 0) for step in steps])
        return kept + came.astype(jnp.float32)

    groups = lax.optimization_barrier((across(given_steps), across(kept_steps)))
    came = [swap(group, 2) for group in groups]
    line = [swap(own_spins, 4 * step) for step in range(1, n_line)]
    given_sums = added(given_steps, came[0]).astype(jnp.bfloat16)
    passed = swap(given_sums, 4)
    came_kept, _ = lax.optimization_barrier((came[1], given_sums))
    line, _ = lax.optimization_barrier((line, came_kept))
    kept_sums = added(kept_steps, came_kept)
    line_spins = jnp.zeros((n_line, sub_len, batch), jnp.bfloat16)
    for index, block in zip(where["line"], [own_spins] + line):
        line_spins = put_at(line_spins, block[None], index)
    near_spins, peer_line = swap(line_spins, 2), swap(line_spins, 1)
    kept_sums = kept_sums + passed.astype(jnp.float32)
    pieces = [
        swap(kept_sums[step].astype(jnp.bfloat16), 8 * step) for step in range(1, n_high)
    ]
    total = kept_sums[0]
    pieces, peer_line = lax.optimization_barrier((pieces, peer_line))
    for piece in pieces:
        total = total + piece.astype(jnp.float32)
    row_ids = lax.broadcasted_iota(jnp.int32, couple.shape, 0) - own_start
    col_ids = lax.broadcasted_iota(jnp.int32, couple.shape, 1) - where["item_col"]
    self_weight = jnp.sum(
        jnp.where(row_ids == col_ids, couple.astype(jnp.float32), 0.0), axis=1
    ).reshape(n_resp, sub_len, 1)
    self_weight = take(self_weight, where["source"][0], 0)
    own_spin = own_spins.astype(jnp.float32)
    fields = (total - self_weight * own_spin) * inv_root + bias[0][:, None]
    residual = (0.5 * (own_spin + 1.0) - jax.nn.sigmoid(fields)).astype(jnp.bfloat16)

    far = [swap(residual, 8 * step) for step in range(1, n_high)]
    others = []
    for step in range(1, n_resp):
        ring = [(i, (i + step) % n_resp) for i in range(n_resp)]
        others.append(lax.ppermute(residual, "resp", ring))
    near = [swap(residual, bits) for bits in (2, 4, 6)]
    far, near[:2], near_spins = lax.optimization_barrier((far, near[:2], near_spins))
    all_spins = jnp.zeros((n_line, 2, 2, sub_len, batch), jnp.bfloat16)
    for side, core, group in (
        ("near", "core", line_spins),
        ("near", "other_core", peer_line),
        ("other_near", "core", near_spins),
        ("other_near", "other_core", swap(near_spins, 1)),
    ):
        all_spins = put_at(all_spins, group[:, None, None], 0, where[side], where[core])
    all_spins = all_spins.reshape(n_high, width, batch)
    row_res = jnp.zeros((n_resp, sub_len, batch), jnp.bfloat16)
    for index, block in zip(where["source"], [residual] + others):
        row_res = put_at(row_res, block[None], index)
    row_res = row_res.reshape(item_dev, batch)

    row_ids = lax.broadcasted_iota(jnp.int32, (item_dev, width), 0) - own_start
    col_ids = lax.broadcasted_iota(jnp.int32, (item_dev, width), 1) - where["low_col"]
    on_diag = (row_ids == col_ids) & (row_ids >= 0) & (row_ids < sub_len)

    def product(left, right, step):
        grad = lax.dot_general(left, right, NT, preferred_element_type=jnp.float32)
        return jnp.where(on_diag, 0.0, grad) if step == 0 else grad

    def pick(blocks, step):
        picked = blocks[0]
        for index in range(1, n_high):
            picked = jnp.where(where["is_high"][step][index], blocks[index], picked)
        return picked

    def pick_part(parts, block):
        picked = parts[0]
        for step in range(1, n_high):
            picked = jnp.where(where["is_high"][step][block], parts[step], picked)
        return picked

    couple_blocks = jnp.split(couple, n_high, axis=1)
    noise_blocks = jnp.split(noise[0], n_high, axis=1)
    parts = []
    for step in range(n_high):
        current = pick(couple_blocks, step).astype(jnp.float32)
        shake = pick(noise_blocks, step).astype(jnp.float32)
        mirror = product(row_res, take(all_spins, where["high"][step], 0), step) * inv_root
        base = current + DRIFT * (DATA_RATIO * mirror - current) + NOISE_SCALE * shake

        if step:
            blocks = [far[step - 1]] + [swap(far[step - 1], bits) for bits in (2, 4, 6)]
        else:
            blocks = [residual] + near
        if step == n_high - 1:
            blocks, base, parts = lax.optimization_barrier((blocks, base, parts))
        quad = jnp.zeros((4, sub_len, batch), jnp.bfloat16)
        for index, block in zip(where["quad"], blocks):
            quad = put_at(quad, block[None], index)
        peers = swap(quad, 1)
        all_res = jnp.zeros((4, 2, sub_len, batch), jnp.bfloat16)
        all_res = put_at(all_res, quad[:, None], 0, where["core"])
        all_res = put_at(all_res, peers[:, None], 0, where["other_core"])
        part = product(spins, all_res.reshape(width, batch), step)
        part = base + (DRIFT * DATA_RATIO * inv_root) * part
        parts.append(part.astype(jnp.bfloat16))
    return jnp.concatenate([pick_part(parts, i) for i in range(n_high)], axis=1)[None]


def solution(mesh):
    return jax.shard_map(
        shards,
        mesh=mesh,
        in_specs=(
            P("resp", "item", None),
            P("resp", "item", None),
            P("item", "resp"),
            P(None, "item"),
            P(),
        ),
        out_specs=P("resp", "item", None),
        check_vma=False,
    )
```

```python
import math

import jax
import jax.numpy as jnp
from jax import lax
from jax.sharding import PartitionSpec as P

DRIFT = 0.01
DATA_RATIO = 900.0
NOISE_SCALE = math.sqrt(0.02)
NT = (((1,), (1,)), ((), ()))
TN = (((0,), (0,)), ((), ()))


def shards(coupling, noise, bias, responses, indices):
    couple = coupling[0]
    item_dev = couple.shape[0]
    pool, batch = responses.shape[0], indices.shape[0]
    n_resp = lax.axis_size("resp")
    n_item = lax.axis_size("item")
    sub_len = item_dev // n_resp
    n_line = n_item // 4
    width = 8 * sub_len
    n_high = n_item // 8
    inv_root = 1.0 / math.sqrt(item_dev * n_item)
    resp_idx = lax.axis_index("resp")
    item_idx = lax.axis_index("item")

    core_idx, near_idx, line_idx, high_idx = item_idx % 2, item_idx // 2 % 2, item_idx // 4, item_idx // 8
    where = dict(
        core=core_idx,
        other_core=1 - core_idx,
        near=near_idx,
        other_near=1 - near_idx,
        line=[line_idx ^ step for step in range(n_line)],
        quad=[item_idx // 2 % 4 ^ step for step in range(4)],
        high=[high_idx ^ step for step in range(n_high)],
        source=[(resp_idx - step) % n_resp for step in range(n_resp)],
        own_start=resp_idx * sub_len,
        item_col=item_idx * sub_len,
    )
    indices, where = lax.optimization_barrier((indices, where))
    own_start = where["own_start"]

    def swap(array, bits):
        return lax.ppermute(array, "item", [(i, i ^ bits) for i in range(n_item)])

    def take(array, index, axis):
        return lax.dynamic_index_in_dim(array, index, axis, False, allow_negative_indices=False)

    def put_at(array, part, *starts):
        starts = starts + (0,) * (array.ndim - len(starts))
        return lax.dynamic_update_slice(array, part, starts, allow_negative_indices=False)

    by_core = couple.reshape(item_dev, -1, 2, sub_len)
    kept = take(by_core, where["core"], 2).reshape(item_dev, -1)
    given = take(by_core, where["other_core"], 2).reshape(item_dev, -1)
    got = swap(given, 1)

    pool_ids = lax.broadcasted_iota(jnp.int32, (pool, batch), 0)
    picks = (pool_ids == indices[None]).astype(jnp.bfloat16)
    pool_spins = (2 * responses - 1).astype(jnp.bfloat16)
    spins = lax.dot_general(pool_spins, picks, TN, preferred_element_type=jnp.float32)
    spins = spins.astype(jnp.bfloat16)
    peer_spins = swap(spins, 1)
    own_spins = take(spins.reshape(n_resp, sub_len, batch), where["source"][0], 0)

    partial = lax.dot_general(
        kept, spins, TN, preferred_element_type=jnp.float32
    ) + lax.dot_general(got, peer_spins, TN, preferred_element_type=jnp.float32)

    by_near = partial.reshape(n_line, 2, sub_len, batch)
    sent = take(by_near, where["other_near"], 1).astype(jnp.bfloat16)
    mine = take(by_near, where["near"], 1)
    sent, mine, own_spins = lax.optimization_barrier((sent, mine, own_spins))
    given_steps, kept_steps = list(range(1, n_line, 2)), list(range(0, n_line, 2))

    def across(steps):
        return jnp.stack([take(sent, where["line"][step], 0) for step in steps])

    def added(steps, came):
        kept = jnp.stack([take(mine, where["line"][step], 0) for step in steps])
        return kept + came.astype(jnp.float32)

    groups = lax.optimization_barrier((across(given_steps), across(kept_steps)))
    came = [swap(group, 2) for group in groups]
    line = [swap(own_spins, 4 * step) for step in range(1, n_line)]
    given_sums = added(given_steps, came[0]).astype(jnp.bfloat16)
    passed = swap(given_sums, 4)
    came_kept, _ = lax.optimization_barrier((came[1], given_sums))
    line, _ = lax.optimization_barrier((line, came_kept))
    kept_sums = added(kept_steps, came_kept)
    line_spins = jnp.zeros((n_line, sub_len, batch), jnp.bfloat16)
    for index, block in zip(where["line"], [own_spins] + line):
        line_spins = put_at(line_spins, block[None], index)
    near_spins, peer_line = swap(line_spins, 2), swap(line_spins, 1)
    kept_sums = kept_sums + passed.astype(jnp.float32)
    pieces = [
        swap(kept_sums[step].astype(jnp.bfloat16), 8 * step) for step in range(1, n_high)
    ]
    total = kept_sums[0]
    pieces, peer_line = lax.optimization_barrier((pieces, peer_line))
    for piece in pieces:
        total = total + piece.astype(jnp.float32)
    row_ids = lax.broadcasted_iota(jnp.int32, couple.shape, 0) - own_start
    col_ids = lax.broadcasted_iota(jnp.int32, couple.shape, 1) - where["item_col"]
    self_weight = jnp.sum(
        jnp.where(row_ids == col_ids, couple.astype(jnp.float32), 0.0), axis=1
    ).reshape(n_resp, sub_len, 1)
    self_weight = take(self_weight, where["source"][0], 0)
    own_spin = own_spins.astype(jnp.float32)
    fields = (total - self_weight * own_spin) * inv_root + bias[0][:, None]
    residual = (0.5 * (own_spin + 1.0) - jax.nn.sigmoid(fields)).astype(jnp.bfloat16)

    far = [swap(residual, 8 * step) for step in range(1, n_high)]
    others = []
    for step in range(1, n_resp):
        ring = [(i, (i + step) % n_resp) for i in range(n_resp)]
        others.append(lax.ppermute(residual, "resp", ring))
    near = [swap(residual, bits) for bits in (2, 4, 6)]
    far, near[:2], near_spins = lax.optimization_barrier((far, near[:2], near_spins))
    all_spins = jnp.zeros((n_line, 2, 2, sub_len, batch), jnp.bfloat16)
    for side, core, group in (
        ("near", "core", line_spins),
        ("near", "other_core", peer_line),
        ("other_near", "core", near_spins),
        ("other_near", "other_core", swap(near_spins, 1)),
    ):
        all_spins = put_at(all_spins, group[:, None, None], 0, where[side], where[core])
    all_spins = all_spins.reshape(n_high, width, batch)
    row_res = jnp.zeros((n_resp, sub_len, batch), jnp.bfloat16)
    for index, block in zip(where["source"], [residual] + others):
        row_res = put_at(row_res, block[None], index)
    row_res = row_res.reshape(item_dev, batch)

    row_ids = lax.broadcasted_iota(jnp.int32, couple.shape, 0) - own_start
    col_ids = lax.broadcasted_iota(jnp.int32, couple.shape, 1) - where["item_col"]
    on_diag = (row_ids == col_ids) & (row_ids >= 0) & (row_ids < sub_len)

    def product(left, right):
        right = right.reshape(-1, batch)
        grad = lax.dot_general(left, right, NT, preferred_element_type=jnp.float32)
        return jnp.where(on_diag, 0.0, grad)

    current = couple.astype(jnp.float32)
    base = current + DRIFT * (DATA_RATIO * (product(row_res, all_spins) * inv_root) - current)
    base = base + NOISE_SCALE * noise[0].astype(jnp.float32)

    all_res = jnp.zeros((n_high, 4, 2, sub_len, batch), jnp.bfloat16)
    for step in range(n_high):
        if step:
            blocks = [far[step - 1]] + [swap(far[step - 1], bits) for bits in (2, 4, 6)]
        else:
            blocks = [residual] + near
        if step == n_high - 1:
            blocks, base, all_res = lax.optimization_barrier((blocks, base, all_res))
        quad = jnp.zeros((4, sub_len, batch), jnp.bfloat16)
        for index, block in zip(where["quad"], blocks):
            quad = put_at(quad, block[None], index)
        for core, group in (("core", quad), ("other_core", swap(quad, 1))):
            all_res = put_at(all_res, group[None, :, None], where["high"][step], 0, where[core])
    change = (DRIFT * DATA_RATIO * inv_root) * product(spins, all_res)
    return (base + change).astype(jnp.bfloat16)[None]


def solution(mesh):
    return jax.shard_map(
        shards,
        mesh=mesh,
        in_specs=(
            P("resp", "item", None),
            P("resp", "item", None),
            P("item", "resp"),
            P(None, "item"),
            P(),
        ),
        out_specs=P("resp", "item", None),
        check_vma=False,
    )
```

```python
import math

import jax
import jax.numpy as jnp
from jax import lax
from jax.sharding import PartitionSpec as P

DRIFT = 0.01
DATA_RATIO = 900.0
NOISE_SCALE = math.sqrt(0.02)
NT = (((1,), (1,)), ((), ()))
TN = (((0,), (0,)), ((), ()))


def shards(coupling, noise, bias, responses, indices):
    couple = coupling[0]
    item_dev = couple.shape[0]
    pool, batch = responses.shape[0], indices.shape[0]
    n_resp = lax.axis_size("resp")
    n_item = lax.axis_size("item")
    sub_len = item_dev // n_resp
    n_line = n_item // 4
    width = 8 * sub_len
    n_high = n_item // 8
    inv_root = 1.0 / math.sqrt(item_dev * n_item)
    resp_idx = lax.axis_index("resp")
    item_idx = lax.axis_index("item")

    core_idx, near_idx, line_idx, high_idx = item_idx % 2, item_idx // 2 % 2, item_idx // 4, item_idx // 8
    where = dict(
        core=core_idx,
        other_core=1 - core_idx,
        near=near_idx,
        other_near=1 - near_idx,
        line=[line_idx ^ step for step in range(n_line)],
        quad=[item_idx // 2 % 4 ^ step for step in range(4)],
        high=[high_idx ^ step for step in range(n_high)],
        source=[(resp_idx - step) % n_resp for step in range(n_resp)],
        own_start=resp_idx * sub_len,
        item_col=item_idx * sub_len,
    )
    indices, where = lax.optimization_barrier((indices, where))
    own_start = where["own_start"]

    def swap(array, bits):
        return lax.ppermute(array, "item", [(i, i ^ bits) for i in range(n_item)])

    def take(array, index, axis):
        return lax.dynamic_index_in_dim(array, index, axis, False, allow_negative_indices=False)

    def put_at(array, part, *starts):
        starts = starts + (0,) * (array.ndim - len(starts))
        return lax.dynamic_update_slice(array, part, starts, allow_negative_indices=False)

    by_core = couple.reshape(item_dev, -1, 2, sub_len)
    kept = take(by_core, where["core"], 2).reshape(item_dev, -1)
    given = take(by_core, where["other_core"], 2).reshape(item_dev, -1)
    got = swap(given, 1)

    pool_ids = lax.broadcasted_iota(jnp.int32, (pool, batch), 0)
    picks = (pool_ids == indices[None]).astype(jnp.bfloat16)
    pool_spins = (2 * responses - 1).astype(jnp.bfloat16)
    spins = lax.dot_general(pool_spins, picks, TN, preferred_element_type=jnp.float32)
    spins = spins.astype(jnp.bfloat16)
    peer_spins = swap(spins, 1)
    own_spins = take(spins.reshape(n_resp, sub_len, batch), where["source"][0], 0)

    partial = lax.dot_general(
        kept, spins, TN, preferred_element_type=jnp.float32
    ) + lax.dot_general(got, peer_spins, TN, preferred_element_type=jnp.float32)

    by_near = partial.reshape(n_line, 2, sub_len, batch)
    sent = take(by_near, where["other_near"], 1).astype(jnp.bfloat16)
    mine = take(by_near, where["near"], 1)
    sent, mine, own_spins = lax.optimization_barrier((sent, mine, own_spins))
    given_steps, kept_steps = list(range(1, n_line, 2)), list(range(0, n_line, 2))

    def across(steps):
        return jnp.stack([take(sent, where["line"][step], 0) for step in steps])

    def added(steps, came):
        kept = jnp.stack([take(mine, where["line"][step], 0) for step in steps])
        return kept + came.astype(jnp.float32)

    groups = lax.optimization_barrier((across(given_steps), across(kept_steps)))
    came = [swap(group, 2) for group in groups]
    line = [swap(own_spins, 4 * step) for step in range(1, n_line)]
    given_sums = added(given_steps, came[0]).astype(jnp.bfloat16)
    passed = swap(given_sums, 4)
    came_kept, _ = lax.optimization_barrier((came[1], given_sums))
    line, _ = lax.optimization_barrier((line, came_kept))
    kept_sums = added(kept_steps, came_kept)
    line_spins = jnp.zeros((n_line, sub_len, batch), jnp.bfloat16)
    for index, block in zip(where["line"], [own_spins] + line):
        line_spins = put_at(line_spins, block[None], index)
    near_spins, peer_line = swap(line_spins, 2), swap(line_spins, 1)
    kept_sums = kept_sums + passed.astype(jnp.float32)
    pieces = [
        swap(kept_sums[step].astype(jnp.bfloat16), 8 * step) for step in range(1, n_high)
    ]
    total = kept_sums[0]
    pieces, peer_line = lax.optimization_barrier((pieces, peer_line))
    for piece in pieces:
        total = total + piece.astype(jnp.float32)
    row_ids = lax.broadcasted_iota(jnp.int32, couple.shape, 0) - own_start
    col_ids = lax.broadcasted_iota(jnp.int32, couple.shape, 1) - where["item_col"]
    self_weight = jnp.sum(
        jnp.where(row_ids == col_ids, couple.astype(jnp.float32), 0.0), axis=1
    ).reshape(n_resp, sub_len, 1)
    self_weight = take(self_weight, where["source"][0], 0)
    own_spin = own_spins.astype(jnp.float32)
    fields = (total - self_weight * own_spin) * inv_root + bias[0][:, None]
    residual = (0.5 * (own_spin + 1.0) - jax.nn.sigmoid(fields)).astype(jnp.bfloat16)

    far = [swap(residual, 8 * step) for step in range(1, n_high)]
    others = []
    for step in range(1, n_resp):
        ring = [(i, (i + step) % n_resp) for i in range(n_resp)]
        others.append(lax.ppermute(residual, "resp", ring))
    near = [swap(residual, bits) for bits in (2, 4, 6)]
    near_spins, near[1], near[0], far = lax.optimization_barrier((near_spins, near[1], near[0], far))
    all_spins = jnp.zeros((n_line, 2, 2, sub_len, batch), jnp.bfloat16)
    for side, core, group in (
        ("near", "core", line_spins),
        ("near", "other_core", peer_line),
        ("other_near", "core", near_spins),
        ("other_near", "other_core", swap(near_spins, 1)),
    ):
        all_spins = put_at(all_spins, group[:, None, None], 0, where[side], where[core])
    all_spins = all_spins.reshape(n_high, width, batch)
    row_res = jnp.zeros((n_resp, sub_len, batch), jnp.bfloat16)
    for index, block in zip(where["source"], [residual] + others):
        row_res = put_at(row_res, block[None], index)
    row_res = row_res.reshape(item_dev, batch)

    row_ids = lax.broadcasted_iota(jnp.int32, couple.shape, 0) - own_start
    col_ids = lax.broadcasted_iota(jnp.int32, couple.shape, 1) - where["item_col"]
    on_diag = (row_ids == col_ids) & (row_ids >= 0) & (row_ids < sub_len)

    def product(left, right):
        right = right.reshape(-1, batch)
        grad = lax.dot_general(left, right, NT, preferred_element_type=jnp.float32)
        return jnp.where(on_diag, 0.0, grad)

    current = couple.astype(jnp.float32)
    base = current + DRIFT * (DATA_RATIO * (product(row_res, all_spins) * inv_root) - current)
    base = base + NOISE_SCALE * noise[0].astype(jnp.float32)

    all_res = jnp.zeros((n_high, 4, 2, sub_len, batch), jnp.bfloat16)
    for step in range(n_high):
        if step:
            blocks = [swap(far[step - 1], bits) for bits in (6, 4, 2)] + [far[step - 1]]
        else:
            blocks = near[::-1] + [residual]
        if step == n_high - 1:
            blocks, base, all_res = lax.optimization_barrier((blocks, base, all_res))
        quad = jnp.zeros((4, sub_len, batch), jnp.bfloat16)
        for index, block in zip(where["quad"][::-1], blocks):
            quad = put_at(quad, block[None], index)
        for core, group in (("core", quad), ("other_core", swap(quad, 1))):
            all_res = put_at(all_res, group[None, :, None], where["high"][step], 0, where[core])
    change = (DRIFT * DATA_RATIO * inv_root) * product(spins, all_res)
    return (base + change).astype(jnp.bfloat16)[None]


def solution(mesh):
    return jax.shard_map(
        shards,
        mesh=mesh,
        in_specs=(
            P("resp", "item", None),
            P("resp", "item", None),
            P("item", "resp"),
            P(None, "item"),
            P(),
        ),
        out_specs=P("resp", "item", None),
        check_vma=False,
    )
```

```python
import math

import jax
import jax.numpy as jnp
from jax import lax
from jax.sharding import PartitionSpec as P

DRIFT = 0.01
DATA_RATIO = 900.0
NOISE_SCALE = math.sqrt(0.02)
NT = (((1,), (1,)), ((), ()))
TN = (((0,), (0,)), ((), ()))


def shards(coupling, noise, bias, responses, indices):
    couple = coupling[0]
    item_dev = couple.shape[0]
    pool, batch = responses.shape[0], indices.shape[0]
    n_resp = lax.axis_size("resp")
    n_item = lax.axis_size("item")
    sub_len = item_dev // n_resp
    n_line = n_item // 4
    width = 8 * sub_len
    n_high = n_item // 8
    inv_root = 1.0 / math.sqrt(item_dev * n_item)
    resp_idx = lax.axis_index("resp")
    item_idx = lax.axis_index("item")

    core_idx, near_idx, line_idx, high_idx = item_idx % 2, item_idx // 2 % 2, item_idx // 4, item_idx // 8
    where = dict(
        core=core_idx,
        other_core=1 - core_idx,
        near=near_idx,
        other_near=1 - near_idx,
        line=[line_idx ^ step for step in range(n_line)],
        quad=[item_idx // 2 % 4 ^ step for step in range(4)],
        high=[high_idx ^ step for step in range(n_high)],
        source=[(resp_idx - step) % n_resp for step in range(n_resp)],
        own_start=resp_idx * sub_len,
        item_col=item_idx * sub_len,
    )
    indices, where = lax.optimization_barrier((indices, where))
    own_start = where["own_start"]

    def swap(array, bits):
        return lax.ppermute(array, "item", [(i, i ^ bits) for i in range(n_item)])

    def take(array, index, axis):
        return lax.dynamic_index_in_dim(array, index, axis, False, allow_negative_indices=False)

    def put_at(array, part, *starts):
        starts = starts + (0,) * (array.ndim - len(starts))
        return lax.dynamic_update_slice(array, part, starts, allow_negative_indices=False)

    by_core = couple.reshape(item_dev, -1, 2, sub_len)
    kept = take(by_core, where["core"], 2).reshape(item_dev, -1)
    given = take(by_core, where["other_core"], 2).reshape(item_dev, -1)
    got = swap(given, 1)

    pool_ids = lax.broadcasted_iota(jnp.int32, (pool, batch), 0)
    picks = (pool_ids == indices[None]).astype(jnp.bfloat16)
    pool_spins = (2 * responses - 1).astype(jnp.bfloat16)
    spins = lax.dot_general(pool_spins, picks, TN, preferred_element_type=jnp.float32)
    spins = spins.astype(jnp.bfloat16)
    peer_spins = swap(spins, 1)
    own_spins = take(spins.reshape(n_resp, sub_len, batch), where["source"][0], 0)

    partial = lax.dot_general(
        kept, spins, TN, preferred_element_type=jnp.float32
    ) + lax.dot_general(got, peer_spins, TN, preferred_element_type=jnp.float32)

    by_near = partial.reshape(n_line, 2, sub_len, batch)
    sent = take(by_near, where["other_near"], 1).astype(jnp.bfloat16)
    mine = take(by_near, where["near"], 1)
    sent, mine, own_spins = lax.optimization_barrier((sent, mine, own_spins))
    given_steps, kept_steps = list(range(1, n_line, 2)), list(range(0, n_line, 2))

    def across(steps):
        return jnp.stack([take(sent, where["line"][step], 0) for step in steps])

    def added(steps, came):
        kept = jnp.stack([take(mine, where["line"][step], 0) for step in steps])
        return kept + came.astype(jnp.float32)

    groups = lax.optimization_barrier((across(given_steps), across(kept_steps)))
    came = [swap(group, 2) for group in groups]
    line = [swap(own_spins, 4 * step) for step in range(1, n_line)]
    given_sums = added(given_steps, came[0]).astype(jnp.bfloat16)
    passed = swap(given_sums, 4)
    came_kept, _ = lax.optimization_barrier((came[1], given_sums))
    line, _ = lax.optimization_barrier((line, came_kept))
    kept_sums = added(kept_steps, came_kept)
    line_spins = jnp.zeros((n_line, sub_len, batch), jnp.bfloat16)
    for index, block in zip(where["line"], [own_spins] + line):
        line_spins = put_at(line_spins, block[None], index)
    near_spins, peer_line = swap(line_spins, 2), swap(line_spins, 1)
    kept_sums = kept_sums + passed.astype(jnp.float32)
    pieces = [
        swap(kept_sums[step].astype(jnp.bfloat16), 8 * step) for step in range(1, n_high)
    ]
    total = kept_sums[0]
    pieces, peer_line = lax.optimization_barrier((pieces, peer_line))
    for piece in pieces:
        total = total + piece.astype(jnp.float32)
    row_ids = lax.broadcasted_iota(jnp.int32, couple.shape, 0) - own_start
    col_ids = lax.broadcasted_iota(jnp.int32, couple.shape, 1) - where["item_col"]
    self_weight = jnp.sum(
        jnp.where(row_ids == col_ids, couple.astype(jnp.float32), 0.0), axis=1
    ).reshape(n_resp, sub_len, 1)
    self_weight = take(self_weight, where["source"][0], 0)
    own_spin = own_spins.astype(jnp.float32)
    fields = (total - self_weight * own_spin) * inv_root + bias[0][:, None]
    residual = (0.5 * (own_spin + 1.0) - jax.nn.sigmoid(fields)).astype(jnp.bfloat16)

    far = [swap(residual, 8 * step) for step in range(1, n_high)]
    others = []
    for step in range(1, n_resp):
        ring = [(i, (i + step) % n_resp) for i in range(n_resp)]
        others.append(lax.ppermute(residual, "resp", ring))
    near = [swap(residual, bits) for bits in (2, 4, 6)]
    near_spins, near[0], near[1], far = lax.optimization_barrier((near_spins, near[0], near[1], far))
    all_spins = jnp.zeros((n_line, 2, 2, sub_len, batch), jnp.bfloat16)
    for side, core, group in (
        ("near", "core", line_spins),
        ("near", "other_core", peer_line),
        ("other_near", "core", near_spins),
        ("other_near", "other_core", swap(near_spins, 1)),
    ):
        all_spins = put_at(all_spins, group[:, None, None], 0, where[side], where[core])
    all_spins = all_spins.reshape(n_high, width, batch)
    row_res = jnp.zeros((n_resp, sub_len, batch), jnp.bfloat16)
    for index, block in zip(where["source"], [residual] + others):
        row_res = put_at(row_res, block[None], index)
    row_res = row_res.reshape(item_dev, batch)

    row_ids = lax.broadcasted_iota(jnp.int32, couple.shape, 0) - own_start
    col_ids = lax.broadcasted_iota(jnp.int32, couple.shape, 1) - where["item_col"]
    on_diag = (row_ids == col_ids) & (row_ids >= 0) & (row_ids < sub_len)

    def product(left, right):
        right = right.reshape(-1, batch)
        grad = lax.dot_general(left, right, NT, preferred_element_type=jnp.float32)
        return jnp.where(on_diag, 0.0, grad)

    current = couple.astype(jnp.float32)
    base = current + DRIFT * (DATA_RATIO * (product(row_res, all_spins) * inv_root) - current)
    base = base + NOISE_SCALE * noise[0].astype(jnp.float32)

    all_res = jnp.zeros((n_high, 4, 2, sub_len, batch), jnp.bfloat16)
    for step in range(n_high):
        if step:
            blocks = [swap(far[step - 1], bits) for bits in (6, 4, 2)] + [far[step - 1]]
        else:
            blocks = near[::-1] + [residual]
        if step == n_high - 1:
            blocks, base, all_res = lax.optimization_barrier((blocks, base, all_res))
        quad = jnp.zeros((4, sub_len, batch), jnp.bfloat16)
        for index, block in zip(where["quad"][::-1], blocks):
            quad = put_at(quad, block[None], index)
        for core, group in (("core", quad), ("other_core", swap(quad, 1))):
            all_res = put_at(all_res, group[None, :, None], where["high"][step], 0, where[core])
    change = (DRIFT * DATA_RATIO * inv_root) * product(spins, all_res)
    return (base + change).astype(jnp.bfloat16)[None]


def solution(mesh):
    return jax.shard_map(
        shards,
        mesh=mesh,
        in_specs=(
            P("resp", "item", None),
            P("resp", "item", None),
            P("item", "resp"),
            P(None, "item"),
            P(),
        ),
        out_specs=P("resp", "item", None),
        check_vma=False,
    )
```

```python
import math

import jax
import jax.numpy as jnp
from jax import lax
from jax.sharding import PartitionSpec as P

DRIFT = 0.01
DATA_RATIO = 900.0
NOISE_SCALE = math.sqrt(0.02)
NT = (((1,), (1,)), ((), ()))
TN = (((0,), (0,)), ((), ()))


def shards(coupling, noise, bias, responses, indices):
    couple = coupling[0]
    item_dev = couple.shape[0]
    pool, batch = responses.shape[0], indices.shape[0]
    n_resp = lax.axis_size("resp")
    n_item = lax.axis_size("item")
    sub_len = item_dev // n_resp
    n_line = n_item // 4
    width = 8 * sub_len
    n_high = n_item // 8
    inv_root = 1.0 / math.sqrt(item_dev * n_item)
    resp_idx = lax.axis_index("resp")
    item_idx = lax.axis_index("item")

    core_idx, near_idx, line_idx, high_idx = item_idx % 2, item_idx // 2 % 2, item_idx // 4, item_idx // 8
    where = dict(
        core=core_idx,
        other_core=1 - core_idx,
        near=near_idx,
        other_near=1 - near_idx,
        line=[line_idx ^ step for step in range(n_line)],
        quad=[item_idx // 2 % 4 ^ step for step in range(4)],
        high=[high_idx ^ step for step in range(n_high)],
        source=[(resp_idx - step) % n_resp for step in range(n_resp)],
        own_start=resp_idx * sub_len,
        item_col=item_idx * sub_len,
    )
    indices, where = lax.optimization_barrier((indices, where))
    own_start = where["own_start"]

    def swap(array, bits):
        return lax.ppermute(array, "item", [(i, i ^ bits) for i in range(n_item)])

    def take(array, index, axis):
        return lax.dynamic_index_in_dim(array, index, axis, False, allow_negative_indices=False)

    def put_at(array, part, *starts):
        starts = starts + (0,) * (array.ndim - len(starts))
        return lax.dynamic_update_slice(array, part, starts, allow_negative_indices=False)

    by_core = couple.reshape(item_dev, -1, 2, sub_len)
    kept = take(by_core, where["core"], 2).reshape(item_dev, -1)
    given = take(by_core, where["other_core"], 2).reshape(item_dev, -1)
    got = swap(given, 1)

    pool_ids = lax.broadcasted_iota(jnp.int32, (pool, batch), 0)
    picks = (pool_ids == indices[None]).astype(jnp.bfloat16)
    pool_spins = (2 * responses - 1).astype(jnp.bfloat16)
    spins = lax.dot_general(pool_spins, picks, TN, preferred_element_type=jnp.float32)
    spins = spins.astype(jnp.bfloat16)
    peer_spins = swap(spins, 1)
    own_spins = take(spins.reshape(n_resp, sub_len, batch), where["source"][0], 0)

    partial = lax.dot_general(
        kept, spins, TN, preferred_element_type=jnp.float32
    ) + lax.dot_general(got, peer_spins, TN, preferred_element_type=jnp.float32)

    by_near = partial.reshape(n_line, 2, sub_len, batch)
    sent = take(by_near, where["other_near"], 1).astype(jnp.bfloat16)
    mine = take(by_near, where["near"], 1)
    sent, mine, own_spins = lax.optimization_barrier((sent, mine, own_spins))
    given_steps, kept_steps = list(range(1, n_line, 2)), list(range(0, n_line, 2))

    def across(steps):
        return jnp.stack([take(sent, where["line"][step], 0) for step in steps])

    def added(steps, came):
        kept = jnp.stack([take(mine, where["line"][step], 0) for step in steps])
        return kept + came.astype(jnp.float32)

    groups = lax.optimization_barrier((across(given_steps), across(kept_steps)))
    came = [swap(group, 2) for group in groups]
    line = [swap(own_spins, 4 * step) for step in range(1, n_line)]
    given_sums = added(given_steps, came[0]).astype(jnp.bfloat16)
    passed = swap(given_sums, 4)
    came_kept, _ = lax.optimization_barrier((came[1], given_sums))
    line, _ = lax.optimization_barrier((line, given_sums))
    kept_sums = added(kept_steps, came_kept)
    line_spins = jnp.zeros((n_line, sub_len, batch), jnp.bfloat16)
    for index, block in zip(where["line"], [own_spins] + line):
        line_spins = put_at(line_spins, block[None], index)
    near_spins, peer_line = swap(line_spins, 2), swap(line_spins, 1)
    kept_sums = kept_sums + passed.astype(jnp.float32)
    pieces = [
        swap(kept_sums[step].astype(jnp.bfloat16), 8 * step) for step in range(1, n_high)
    ]
    total = kept_sums[0]
    pieces, peer_line = lax.optimization_barrier((pieces, peer_line))
    for piece in pieces:
        total = total + piece.astype(jnp.float32)
    row_ids = lax.broadcasted_iota(jnp.int32, couple.shape, 0) - own_start
    col_ids = lax.broadcasted_iota(jnp.int32, couple.shape, 1) - where["item_col"]
    self_weight = jnp.sum(
        jnp.where(row_ids == col_ids, couple.astype(jnp.float32), 0.0), axis=1
    ).reshape(n_resp, sub_len, 1)
    self_weight = take(self_weight, where["source"][0], 0)
    own_spin = own_spins.astype(jnp.float32)
    fields = (total - self_weight * own_spin) * inv_root + bias[0][:, None]
    residual = (0.5 * (own_spin + 1.0) - jax.nn.sigmoid(fields)).astype(jnp.bfloat16)

    far = [swap(residual, 8 * step) for step in range(1, n_high)]
    others = []
    for step in range(1, n_resp):
        ring = [(i, (i + step) % n_resp) for i in range(n_resp)]
        others.append(lax.ppermute(residual, "resp", ring))
    near = [swap(residual, bits) for bits in (2, 4, 6)]
    near_spins, near[0], near[1], far = lax.optimization_barrier((near_spins, near[0], near[1], far))
    all_spins = jnp.zeros((n_line, 2, 2, sub_len, batch), jnp.bfloat16)
    for side, core, group in (
        ("near", "core", line_spins),
        ("near", "other_core", peer_line),
        ("other_near", "core", near_spins),
        ("other_near", "other_core", swap(near_spins, 1)),
    ):
        all_spins = put_at(all_spins, group[:, None, None], 0, where[side], where[core])
    all_spins = all_spins.reshape(n_high, width, batch)
    row_res = jnp.zeros((n_resp, sub_len, batch), jnp.bfloat16)
    for index, block in zip(where["source"], [residual] + others):
        row_res = put_at(row_res, block[None], index)
    row_res = row_res.reshape(item_dev, batch)

    row_ids = lax.broadcasted_iota(jnp.int32, couple.shape, 0) - own_start
    col_ids = lax.broadcasted_iota(jnp.int32, couple.shape, 1) - where["item_col"]
    on_diag = (row_ids == col_ids) & (row_ids >= 0) & (row_ids < sub_len)

    def product(left, right):
        right = right.reshape(-1, batch)
        grad = lax.dot_general(left, right, NT, preferred_element_type=jnp.float32)
        return jnp.where(on_diag, 0.0, grad)

    current = couple.astype(jnp.float32)
    base = current + DRIFT * (DATA_RATIO * (product(row_res, all_spins) * inv_root) - current)
    base = base + NOISE_SCALE * noise[0].astype(jnp.float32)

    all_res = jnp.zeros((n_high, 4, 2, sub_len, batch), jnp.bfloat16)
    for step in range(n_high):
        if step:
            blocks = [swap(far[step - 1], bits) for bits in (6, 4, 2)] + [far[step - 1]]
        else:
            blocks = near[::-1] + [residual]
        if step == n_high - 1:
            blocks, base, all_res = lax.optimization_barrier((blocks, base, all_res))
        quad = jnp.zeros((4, sub_len, batch), jnp.bfloat16)
        for index, block in zip(where["quad"][::-1], blocks):
            quad = put_at(quad, block[None], index)
        for core, group in (("core", quad), ("other_core", swap(quad, 1))):
            all_res = put_at(all_res, group[None, :, None], where["high"][step], 0, where[core])
    change = (DRIFT * DATA_RATIO * inv_root) * product(spins, all_res)
    return (base + change).astype(jnp.bfloat16)[None]


def solution(mesh):
    return jax.shard_map(
        shards,
        mesh=mesh,
        in_specs=(
            P("resp", "item", None),
            P("resp", "item", None),
            P("item", "resp"),
            P(None, "item"),
            P(),
        ),
        out_specs=P("resp", "item", None),
        check_vma=False,
    )
```
